32 devices in a mesh: sensor: 16 (over z, x, core), day: 2 (over y).
Axes of the slice: x: 2, y: 2, z: 4, core: 2. Of those that a mesh axis runs over, the one named last changes fastest.
Arguments:
- traffic: bfloat16 [4096, 16384], P('sensor', 'day'), may hold values from -24 to 24
- start_basis: float32 [512, 64], replicated, may hold values from -6 to 6
Outputs:
- day_basis: float32 [512, 64], replicated
- core: bfloat16 [4096, 2048], P(('sensor', 'day'))
The draws below stay inside these ranges and needn't reach their ends.
All inputs are finite; a program needn't handle non-finite values.
Results may differ from the reference program's by a relative error of at most 0.001.
The reference program's roundings to bfloat16 on the way count: a program that leaves them out, or rounds other values in their place, can miss the bound.
Values may be sent and summed in bfloat16 or wider, within the bound.
No kernel may reach another device: no remote copies, remote signals or barrier semaphores. Data moves between devices by JAX's collectives and lax.ppermute only.
A program may use at most 64 MiB of HBM per device.

```python
import math
import jax
import jax.numpy as jnp
from jax import lax

RT = 32
DAYS = 512
RANK = 64
ITERS = 3
SENSORS = 4096
N_SENSOR = 16


def draw_traffic(key, part):
    keys = jax.random.split(jax.random.fold_in(key, 11), 4)
    noise = jax.random.normal(keys[0], (SENSORS, RT, DAYS), jnp.float32)
    column = jnp.exp(jax.random.uniform(keys[1], (DAYS,), jnp.float32, 0.0, math.log(3.0)))
    loads = jax.random.normal(keys[2], (SENSORS, RT, 4), jnp.float32)
    shapes = 0.7 * jax.random.normal(keys[3], (4, DAYS), jnp.float32)
    result = noise * column
    result = result + loads[:, :, 0:1] * shapes[0] + loads[:, :, 1:2] * shapes[1]
    result = result + loads[:, :, 2:3] * shapes[2] + loads[:, :, 3:4] * shapes[3]
    result = jnp.clip(result, -24.0, 24.0)
    result = jnp.transpose(result, (0, 2, 1)).reshape(SENSORS, DAYS * RT)
    return result.astype(jnp.bfloat16)


def normal_values(key, shape, deviation, most, dtype=jnp.bfloat16):
    return jnp.clip(deviation * jax.random.normal(key, shape, jnp.float32), -most, most).astype(dtype)


def setup_inputs(seed: int = 0) -> dict:
    seeds = jax.random.split(jax.random.key(seed), 3)
    traffic = draw_traffic(jax.random.fold_in(seeds[2], 71), 0)
    start_basis = normal_values(seeds[1], (DAYS, RANK), 1.0, 6.0, jnp.float32)
    return dict(traffic=traffic, start_basis=start_basis)


def orthonormalize(images):
    product = jnp.dot(images.T, images, precision=lax.Precision.HIGHEST)
    lower = jnp.linalg.cholesky(product)
    return jax.scipy.linalg.solve_triangular(lower, images.T, lower=True).T

def reference(traffic, start_basis):
    blocks = N_SENSOR
    stacked = traffic.reshape(blocks, SENSORS // blocks, DAYS, RT)

    def add_block(total, block):
        wide = block.astype(jnp.float32)
        return (total + jnp.einsum('sdt,set->de', wide, wide, precision=lax.Precision.HIGHEST), None)
    gram, unused = lax.scan(add_block, jnp.zeros((DAYS, DAYS), jnp.float32), stacked)
    basis = start_basis
    for iteration in range(ITERS):
        images = jnp.dot(gram, basis, precision=lax.Precision.HIGHEST)
        basis = orthonormalize(images)
    day_basis = basis * jnp.sqrt(jnp.float32(DAYS))
    basis_low = basis.astype(jnp.bfloat16)
    basis_wide = basis_low.astype(jnp.float32)

    def project(block):
        result = jnp.einsum('sdt,dr->str', block.astype(jnp.float32), basis_wide, precision=lax.Precision.HIGHEST)
        return result.astype(jnp.bfloat16)
    core = lax.map(project, stacked).reshape(SENSORS, RT * RANK)
    return (day_basis, core)
```

```python
import jax
import jax.numpy as jnp
from jax import lax
from jax.sharding import PartitionSpec as P

ITERS = 3


def orthonormalize(images):
    product = jnp.dot(images.T, images, precision=lax.Precision.HIGHEST)
    lower = jnp.linalg.cholesky(product)
    return jax.scipy.linalg.solve_triangular(lower, images.T, lower=True).T


def sum_over_devices(local, axes):
    devices = lax.axis_size(axes)
    pieces = local.reshape(devices, local.size // devices // 128, 128)
    piece = jnp.sum(lax.all_to_all(pieces, axes, split_axis=0, concat_axis=0, tiled=True), axis=0)
    copies = jnp.broadcast_to(piece, (devices, *piece.shape))
    whole = lax.all_to_all(copies, axes, split_axis=0, concat_axis=0, tiled=True)
    return whole.reshape(local.shape)


def shards(traffic, start_basis):
    regrouped = lax.all_to_all(traffic, "day", split_axis=0, concat_axis=1, tiled=True)
    sensors_here = regrouped.shape[0]
    days_all = start_basis.shape[0]
    components = regrouped.shape[1] // days_all
    series = regrouped.reshape(sensors_here, days_all, components)
    gram_local = lax.dot_general(
        series, series, (((0, 2), (0, 2)), ((), ())), preferred_element_type=jnp.float32
    )
    basis = start_basis
    gram = sum_over_devices(gram_local, ("sensor", "day"))
    for iteration in range(ITERS):
        basis = orthonormalize(jnp.dot(gram, basis, precision=lax.Precision.HIGHEST))
    day_basis = basis * jnp.sqrt(jnp.float32(days_all))
    basis_low = basis.astype(jnp.bfloat16)
    core = jnp.einsum("sdt,dr->str", series, basis_low, preferred_element_type=jnp.float32).astype(
        jnp.bfloat16
    )
    return (day_basis, core.reshape(sensors_here, components * basis_low.shape[1]))


def solution(mesh):
    placed = (P("sensor", "day"), P())
    return jax.shard_map(
        shards,
        mesh=mesh,
        in_specs=placed,
        out_specs=(P(), P(("sensor", "day"), None)),
        check_vma=False,
    )
```

```python
import functools

import jax
import jax.numpy as jnp
from jax import lax
from jax.experimental import pallas as pl
from jax.experimental.pallas import tpu as pltpu
from jax.sharding import PartitionSpec as P

ITERS = 3
AXES = ("sensor", "day")


def dot32(left, right, dims):
    return lax.dot_general(
        left,
        right,
        (dims, ((), ())),
        precision=lax.Precision.HIGHEST,
        preferred_element_type=jnp.float32,
    )


def inverse_factor(product, width=8):
    rank = product.shape[0]
    rows_at = lax.broadcasted_iota(jnp.int32, (rank, rank), 0)
    lanes_at = lax.broadcasted_iota(jnp.int32, (rank, rank), 1)
    unit = jnp.where(rows_at == lanes_at, 1.0, 0.0).astype(jnp.float32)
    both = jnp.concatenate([product, unit], axis=1)
    panels = [both[at : at + width] for at in range(0, rank, width)]
    row_of = lax.broadcasted_iota(jnp.int32, (width, 2 * rank), 0)

    def spread(values):
        return jnp.broadcast_to(values, (width, 2 * rank))

    done = []
    for here in range(rank // width):
        base = here * width
        below = range(here + 1, rank // width)
        rows = [spread(panels[here][w : w + 1]) for w in range(width)]
        pivots = {
            (v, w): spread(rows[v][:, base + w : base + w + 1])
            for v in range(width)
            for w in range(v, width)
        }
        columns = {
            (i, w): spread(panels[i][:, base + w : base + w + 1])
            for i in below
            for w in range(width)
        }
        for v in range(width):
            scale = lax.rsqrt(pivots[v, v])
            rows[v] = rows[v] * scale
            for w in range(v + 1, width):
                pivots[v, w] = pivots[v, w] * scale
            for i in below:
                columns[i, v] = columns[i, v] * scale
            for w in range(v + 1, width):
                for x in range(w, width):
                    pivots[w, x] = pivots[w, x] - pivots[v, w] * pivots[v, x]
                rows[w] = rows[w] - pivots[v, w] * rows[v]
                for i in below:
                    columns[i, w] = columns[i, w] - pivots[v, w] * columns[i, v]
            for i in below:
                panels[i] = panels[i] - columns[i, v] * rows[v]
        panel = rows[0]
        for w in range(1, width):
            panel = jnp.where(row_of == w, rows[w], panel)
        done.append(panel)
    return jnp.concatenate(done, axis=0)[:, rank:]


def rounds_kernel(gram_ref, start_ref, day_basis_ref, low_ref):
    def one_round(_, basis):
        images = dot32(basis, gram_ref[...], ((1,), (0,)))
        product = dot32(images, images, ((1,), (1,)))
        return dot32(inverse_factor(product), images, ((1,), (0,)))

    basis = lax.fori_loop(0, ITERS, one_round, start_ref[...])
    day_basis_ref[...] = basis * jnp.sqrt(jnp.float32(basis.shape[1]))
    low_ref[...] = basis.astype(jnp.bfloat16)


def rounds(gram, start):
    rank, days = start.shape
    whole = pl.BlockSpec(memory_space=pltpu.VMEM)
    return pl.pallas_call(
        rounds_kernel,
        out_shape=(
            jax.ShapeDtypeStruct((rank, days), jnp.float32),
            jax.ShapeDtypeStruct((rank, days), jnp.bfloat16),
        ),
        in_specs=[whole, whole],
        out_specs=(whole, whole),
        name="rounds",
    )(gram, start)


def sum_over_devices(local, axes):
    devices = lax.axis_size(axes)
    pieces = local.reshape(devices, local.size // devices // 128, 128)
    piece = jnp.sum(lax.all_to_all(pieces, axes, split_axis=0, concat_axis=0, tiled=True), axis=0)
    copies = jnp.broadcast_to(piece, (devices, *piece.shape))
    whole = lax.all_to_all(copies, axes, split_axis=0, concat_axis=0, tiled=True)
    return whole.reshape(local.shape)


def shards(traffic, start_basis):
    regrouped = lax.all_to_all(traffic, "day", split_axis=0, concat_axis=1, tiled=True)
    sensors_here = regrouped.shape[0]
    days_all = start_basis.shape[0]
    components = regrouped.shape[1] // days_all
    series = regrouped.reshape(sensors_here, days_all, components)
    gram_local = lax.dot_general(
        series, series, (((0, 2), (0, 2)), ((), ())), preferred_element_type=jnp.float32
    )
    gram = sum_over_devices(gram_local, AXES)
    day_basis, basis_low = rounds(gram, start_basis.T)
    core = jnp.einsum("sdt,rd->str", series, basis_low, preferred_element_type=jnp.float32).astype(
        jnp.bfloat16
    )
    return (day_basis.T, core.reshape(sensors_here, components * basis_low.shape[0]))


def solution(mesh):
    placed = (P("sensor", "day"), P())
    return jax.shard_map(
        shards,
        mesh=mesh,
        in_specs=placed,
        out_specs=(P(), P(AXES, None)),
        check_vma=False,
    )
```

```python
import functools

import jax
import jax.numpy as jnp
from jax import lax
from jax.experimental import pallas as pl
from jax.experimental.pallas import tpu as pltpu
from jax.sharding import PartitionSpec as P

ITERS = 3
AXES = ("sensor", "day")


def dot32(left, right, dims):
    return lax.dot_general(
        left,
        right,
        (dims, ((), ())),
        precision=lax.Precision.HIGHEST,
        preferred_element_type=jnp.float32,
    )


def inverse_factor(product, width=8):
    rank = product.shape[0]
    rows_at = lax.broadcasted_iota(jnp.int32, (rank, rank), 0)
    lanes_at = lax.broadcasted_iota(jnp.int32, (rank, rank), 1)
    unit = jnp.where(rows_at == lanes_at, 1.0, 0.0).astype(jnp.float32)
    both = jnp.concatenate([product, unit], axis=1)
    panels = [both[at : at + width] for at in range(0, rank, width)]
    row_of = lax.broadcasted_iota(jnp.int32, (width, 2 * rank), 0)

    def spread(values):
        return jnp.broadcast_to(values, (width, 2 * rank))

    done = []
    for here in range(rank // width):
        base = here * width
        below = range(here + 1, rank // width)
        rows = [spread(panels[here][w : w + 1]) for w in range(width)]
        pivots = {
            (v, w): spread(rows[v][:, base + w : base + w + 1])
            for v in range(width)
            for w in range(v, width)
        }
        columns = {
            (i, w): spread(panels[i][:, base + w : base + w + 1])
            for i in below
            for w in range(width)
        }
        for v in range(width):
            scale = lax.rsqrt(pivots[v, v])
            rows[v] = rows[v] * scale
            for w in range(v + 1, width):
                pivots[v, w] = pivots[v, w] * scale
            for i in below:
                columns[i, v] = columns[i, v] * scale
            for w in range(v + 1, width):
                for x in range(w, width):
                    pivots[w, x] = pivots[w, x] - pivots[v, w] * pivots[v, x]
                rows[w] = rows[w] - pivots[v, w] * rows[v]
                for i in below:
                    columns[i, w] = columns[i, w] - pivots[v, w] * columns[i, v]
            for i in below:
                panels[i] = panels[i] - columns[i, v] * rows[v]
        panel = rows[0]
        for w in range(1, width):
            panel = jnp.where(row_of == w, rows[w], panel)
        done.append(panel)
    return jnp.concatenate(done, axis=0)[:, rank:]


def one_round(gram_ref, basis):
    images = dot32(basis, gram_ref[...], ((1,), (0,)))
    product = dot32(images, images, ((1,), (1,)))
    return dot32(inverse_factor(product), images, ((1,), (0,)))


def finish(basis, day_basis_ref, low_ref):
    day_basis_ref[...] = basis * jnp.sqrt(jnp.float32(basis.shape[1]))
    low_ref[...] = basis.astype(jnp.bfloat16)


def rounds_kernel(gram_ref, start_ref, day_basis_ref, low_ref):
    basis = lax.fori_loop(0, ITERS, lambda _, b: one_round(gram_ref, b), start_ref[...])
    finish(basis, day_basis_ref, low_ref)


def pieces_rounds_kernel(sensor, own, pieces_ref, start_ref, day_basis_ref, low_ref, gram_ref):
    half = gram_ref.shape[0] // 2
    side = half // 2
    for day in range(2):
        packed = jnp.concatenate([pieces_ref[2 * s + day, :own] for s in range(sensor)], axis=0)
        first, cross, second = packed[:side], packed[side : 2 * side], packed[2 * side :]
        at = day * half
        gram_ref[at : at + side, at : at + side] = first
        gram_ref[at + side : at + half, at : at + side] = cross
        gram_ref[at : at + side, at + side : at + half] = cross.T
        gram_ref[at + side : at + half, at + side : at + half] = second
    off = jnp.concatenate([pieces_ref[d, own:] for d in range(2 * sensor)], axis=0)
    for part in range(2):
        block = off[part * half : (part + 1) * half]
        gram_ref[:half, half + part * side : half + (part + 1) * side] = block
        gram_ref[half + part * side : half + (part + 1) * side, :half] = block.T
    basis = lax.fori_loop(0, ITERS, lambda _, b: one_round(gram_ref, b), start_ref[...])
    finish(basis, day_basis_ref, low_ref)


WHOLE = pl.BlockSpec(memory_space=pltpu.VMEM)
VMEM_LIMIT = 24 * 1024 * 1024


def basis_shapes(start):
    return (
        jax.ShapeDtypeStruct(start.shape, jnp.float32),
        jax.ShapeDtypeStruct(start.shape, jnp.bfloat16),
    )


def rounds(gram, start):
    return pl.pallas_call(
        rounds_kernel,
        out_shape=basis_shapes(start),
        in_specs=[WHOLE, WHOLE],
        out_specs=(WHOLE, WHOLE),
        name="rounds",
    )(gram, start)


def pieces_rounds(pieces, own, start):
    days = start.shape[1]
    return pl.pallas_call(
        functools.partial(pieces_rounds_kernel, pieces.shape[0] // 2, own),
        out_shape=basis_shapes(start),
        in_specs=[WHOLE, WHOLE],
        out_specs=(WHOLE, WHOLE),
        scratch_shapes=[pltpu.VMEM((days, days), jnp.float32)],
        compiler_params=pltpu.CompilerParams(vmem_limit_bytes=VMEM_LIMIT),
        name="rounds",
    )(pieces, start)


GROUP = 8


def components_first(traffic, components, put):
    width = GROUP * components
    sensors = traffic.shape[0]
    row = lax.broadcasted_iota(jnp.int32, (width, width), 0)
    lane = lax.broadcasted_iota(jnp.int32, (width, width), 1)
    order = (row % GROUP) * components + row // GROUP == lane
    order = jnp.where(order, 1.0, 0.0).astype(jnp.bfloat16)
    for pair in range(traffic.shape[1] // (2 * width)):
        parts = []
        for at in (2 * pair * width, (2 * pair + 1) * width):
            turned = lax.dot_general(
                order,
                traffic[:, at : at + width],
                (((1,), (1,)), ((), ())),
                preferred_element_type=jnp.float32,
            )
            parts.append(turned.reshape(components, GROUP, sensors))
        put(2 * GROUP * pair, jnp.concatenate(parts, axis=1).astype(jnp.bfloat16))


def paired_dot(left_ref, right_ref):
    components, _, sensors = left_ref.shape
    step = max(1, 256 // sensors)
    total = None
    for at in range(0, components, step):
        left, right = (
            jnp.concatenate([ref[c] for c in range(at, at + step)], axis=1)
            for ref in (left_ref, right_ref)
        )
        term = lax.dot_general(
            left, right, (((1,), (1,)), ((), ())), preferred_element_type=jnp.float32
        )
        total = term if total is None else total + term
    return total


def local_kernel(traffic_ref, series_ref, packed_ref):
    components = series_ref.shape[0]

    def put(day, values):
        series_ref[:, day : day + values.shape[1], :] = values

    components_first(traffic_ref, components, put)
    gram = paired_dot(series_ref, series_ref)
    side = gram.shape[0] // 2
    packed_ref[:side] = gram[:side, :side]
    packed_ref[side : 2 * side] = gram[side:, :side]
    packed_ref[2 * side :] = gram[side:, side:]


def local(traffic, days, components):
    sensors = traffic.shape[0]
    side = days // 2
    return pl.pallas_call(
        local_kernel,
        out_shape=(
            jax.ShapeDtypeStruct((components, days, sensors), jnp.bfloat16),
            jax.ShapeDtypeStruct((3 * side, side), jnp.float32),
        ),
        in_specs=[WHOLE],
        out_specs=(WHOLE, WHOLE),
        compiler_params=pltpu.CompilerParams(vmem_limit_bytes=VMEM_LIMIT),
        cost_estimate=pl.CostEstimate(
            flops=2 * traffic.size * (days + 256), bytes_accessed=4 * traffic.size, transcendentals=0
        ),
        name="local",
    )(traffic)


def arrived_kernel(before, day_ref, traffic_ref, series_ref, *refs):
    parts, (arrived_ref, gram_ref) = refs[:before], refs[before:]

    def put(day, values):
        arrived_ref[:, day : day + values.shape[1], :] = values

    components_first(traffic_ref, series_ref.shape[0], put)
    gram = paired_dot(arrived_ref, series_ref)
    if gram_ref.shape == gram.shape:
        gram_ref[...] = gram
        return
    gram = jnp.concatenate([*(part[...] for part in parts), gram], axis=0)
    side = gram_ref.shape[1]

    @pl.when(day_ref[0] == 0)
    def _():
        turned = gram.T
        gram_ref[: turned.shape[0]] = turned[:, :side]
        gram_ref[turned.shape[0] :] = turned[:, side:]

    @pl.when(day_ref[0] != 0)
    def _():
        gram_ref[: gram.shape[0]] = gram[:, :side]
        gram_ref[gram.shape[0] :] = gram[:, side:]


def arrived(day, traffic, series, parts, last):
    components, days, _ = series.shape
    sensors = traffic.shape[0]
    here = traffic.shape[1] // components
    gram_shape = (2 * days, days // 2) if last else (here, days)
    grid_spec = pltpu.PrefetchScalarGridSpec(
        num_scalar_prefetch=1,
        grid=(1,),
        in_specs=[
            pl.BlockSpec(traffic.shape, lambda i, day: (0, 0)),
            pl.BlockSpec((components, days, sensors), lambda i, day: (0, 0, day[0])),
            *(pl.BlockSpec(part.shape, lambda i, day: (0, 0)) for part in parts),
        ],
        out_specs=(
            pl.BlockSpec((components, here, sensors), lambda i, day: (0, 0, 0)),
            pl.BlockSpec(gram_shape, lambda i, day: (0, 0)),
        ),
    )
    return pl.pallas_call(
        functools.partial(arrived_kernel, len(parts)),
        grid_spec=grid_spec,
        out_shape=(
            jax.ShapeDtypeStruct((components, here, sensors), jnp.bfloat16),
            jax.ShapeDtypeStruct(gram_shape, jnp.float32),
        ),
        compiler_params=pltpu.CompilerParams(vmem_limit_bytes=VMEM_LIMIT),
        cost_estimate=pl.CostEstimate(
            flops=2 * traffic.size * (days + 256), bytes_accessed=4 * traffic.size, transcendentals=0
        ),
        name="arrived",
    )(day, traffic, series, *parts)


def project_kernel(day_ref, own_basis_ref, other_basis_ref, series_ref, *refs):
    arrived_refs, core_ref = refs[:-1], refs[-1]
    components = series_ref.shape[0]
    rank = own_basis_ref.shape[0]

    def column(c):
        other = jnp.concatenate([ref[c] for ref in arrived_refs], axis=0)
        values = jnp.dot(own_basis_ref[...], series_ref[c], preferred_element_type=jnp.float32)
        values += jnp.dot(other_basis_ref[...], other, preferred_element_type=jnp.float32)
        return values

    step = 128 // rank
    for c in range(0, components, step):
        values = jnp.concatenate([column(c + k) for k in range(step)], axis=0)
        core_ref[:, c * rank : (c + step) * rank] = values.T.astype(jnp.bfloat16)


def project(day, basis, series, parts):
    components, days, _ = series.shape
    sensors = parts[0].shape[2]
    rank = basis.shape[0]
    grid_spec = pltpu.PrefetchScalarGridSpec(
        num_scalar_prefetch=1,
        grid=(1,),
        in_specs=[
            pl.BlockSpec((rank, days), lambda i, day: (0, day[0])),
            pl.BlockSpec((rank, days), lambda i, day: (0, 1 - day[0])),
            pl.BlockSpec((components, days, sensors), lambda i, day: (0, 0, day[0])),
            *(pl.BlockSpec(part.shape, lambda i, day: (0, 0, 0)) for part in parts),
        ],
        out_specs=pl.BlockSpec((sensors, components * rank), lambda i, day: (0, 0)),
    )
    return pl.pallas_call(
        project_kernel,
        grid_spec=grid_spec,
        out_shape=jax.ShapeDtypeStruct((sensors, components * rank), jnp.bfloat16),
        compiler_params=pltpu.CompilerParams(vmem_limit_bytes=VMEM_LIMIT),
        name="project",
    )(day, basis, basis, series, *parts)


def scatter_sum(values, axes):
    devices = lax.axis_size(axes)
    pieces = values.reshape(devices, values.shape[0] // devices, values.shape[1])
    return jnp.sum(lax.all_to_all(pieces, axes, split_axis=0, concat_axis=0, tiled=True), axis=0)


def gather(piece, axes):
    copies = jnp.broadcast_to(piece, (lax.axis_size(axes), *piece.shape))
    return lax.all_to_all(copies, axes, split_axis=0, concat_axis=0, tiled=True)


def sum_over_devices(local, axes):
    flat = local.reshape(local.size // 128, 128)
    return gather(scatter_sum(flat, axes), axes).reshape(local.shape)


def shards(traffic, start_basis):
    regrouped = lax.all_to_all(traffic, "day", split_axis=0, concat_axis=1, tiled=True)
    sensors_here = regrouped.shape[0]
    days_all = start_basis.shape[0]
    components = regrouped.shape[1] // days_all
    series = regrouped.reshape(sensors_here, days_all, components)
    gram_local = lax.dot_general(
        series, series, (((0, 2), (0, 2)), ((), ())), preferred_element_type=jnp.float32
    )
    gram = sum_over_devices(gram_local, AXES)
    day_basis, basis_low = rounds(gram, start_basis.T)
    core = jnp.einsum("sdt,rd->str", series, basis_low, preferred_element_type=jnp.float32).astype(
        jnp.bfloat16
    )
    return (day_basis.T, core.reshape(sensors_here, components * basis_low.shape[0]))


CHUNKS = 4


def paired_shards(traffic, start_basis):
    days = start_basis.shape[0] // 2
    components = traffic.shape[1] // days
    sensors = traffic.shape[0] // 2
    day = lax.axis_index("day")
    swap = [(0, 1), (1, 0)]
    wanted = lax.dynamic_slice_in_dim(traffic, (1 - day) * sensors, sensors, axis=0)
    chunks = [
        lax.ppermute(chunk, "day", swap) for chunk in jnp.split(wanted, CHUNKS, axis=1)
    ]
    series, packed = local(traffic, days, components)
    own = scatter_sum(packed, "sensor")
    index = day.astype(jnp.int32).reshape(1)
    parts, grams = [], []
    for at, chunk in enumerate(chunks):
        last = at == CHUNKS - 1
        part, gram = arrived(index, chunk, series, grams if last else (), last)
        parts.append(part)
        grams.append(gram)
    off = scatter_sum(grams[-1], AXES)
    pieces = gather(jnp.concatenate([own, off], axis=0), AXES)
    day_basis, basis_low = pieces_rounds(pieces, own.shape[0], start_basis.T)
    return (day_basis.T, project(index, basis_low, series, parts))


def pairs(mesh):
    return mesh.shape["day"] == 2


def solution(mesh):
    placed = (P("sensor", "day"), P())
    return jax.shard_map(
        paired_shards if pairs(mesh) else shards,
        mesh=mesh,
        in_specs=placed,
        out_specs=(P(), P(AXES, None)),
        check_vma=False,
    )
```

```python
import functools

import jax
import jax.numpy as jnp
from jax import lax
from jax.experimental import pallas as pl
from jax.experimental.pallas import tpu as pltpu
from jax.sharding import PartitionSpec as P

ITERS = 3
AXES = ("sensor", "day")


def dot32(left, right, dims):
    return lax.dot_general(
        left,
        right,
        (dims, ((), ())),
        precision=lax.Precision.HIGHEST,
        preferred_element_type=jnp.float32,
    )


def inverse_factor(product, width=8):
    rank = product.shape[0]
    rows_at = lax.broadcasted_iota(jnp.int32, (rank, rank), 0)
    lanes_at = lax.broadcasted_iota(jnp.int32, (rank, rank), 1)
    unit = jnp.where(rows_at == lanes_at, 1.0, 0.0).astype(jnp.float32)
    both = jnp.concatenate([product, unit], axis=1)
    panels = [both[at : at + width] for at in range(0, rank, width)]
    row_of = lax.broadcasted_iota(jnp.int32, (width, 2 * rank), 0)

    def spread(values):
        return jnp.broadcast_to(values, (width, 2 * rank))

    done = []
    for here in range(rank // width):
        base = here * width
        below = range(here + 1, rank // width)
        rows = [spread(panels[here][w : w + 1]) for w in range(width)]
        pivots = {
            (v, w): spread(rows[v][:, base + w : base + w + 1])
            for v in range(width)
            for w in range(v, width)
        }
        columns = {
            (i, w): spread(panels[i][:, base + w : base + w + 1])
            for i in below
            for w in range(width)
        }
        for v in range(width):
            scale = lax.rsqrt(pivots[v, v])
            rows[v] = rows[v] * scale
            for w in range(v + 1, width):
                pivots[v, w] = pivots[v, w] * scale
            for i in below:
                columns[i, v] = columns[i, v] * scale
            for w in range(v + 1, width):
                for x in range(w, width):
                    pivots[w, x] = pivots[w, x] - pivots[v, w] * pivots[v, x]
                rows[w] = rows[w] - pivots[v, w] * rows[v]
                for i in below:
                    columns[i, w] = columns[i, w] - pivots[v, w] * columns[i, v]
            for i in below:
                panels[i] = panels[i] - columns[i, v] * rows[v]
        panel = rows[0]
        for w in range(1, width):
            panel = jnp.where(row_of == w, rows[w], panel)
        done.append(panel)
    return jnp.concatenate(done, axis=0)[:, rank:]


def one_round(gram_ref, basis):
    images = dot32(basis, gram_ref[...], ((1,), (0,)))
    product = dot32(images, images, ((1,), (1,)))
    return dot32(inverse_factor(product), images, ((1,), (0,)))


def finish(basis, day_basis_ref, low_ref):
    day_basis_ref[...] = basis * jnp.sqrt(jnp.float32(basis.shape[1]))
    low_ref[...] = basis.astype(jnp.bfloat16)


def rounds_kernel(gram_ref, start_ref, day_basis_ref, low_ref):
    basis = lax.fori_loop(0, ITERS, lambda _, b: one_round(gram_ref, b), start_ref[...])
    finish(basis, day_basis_ref, low_ref)


def join(sensor, own, pieces_ref, gram_ref):
    half = gram_ref.shape[0] // 2
    side = half // 2
    for day in range(2):
        packed = jnp.concatenate([pieces_ref[2 * s + day, :own] for s in range(sensor)], axis=0)
        first, cross, second = packed[:side], packed[side : 2 * side], packed[2 * side :]
        at = day * half
        gram_ref[at : at + side, at : at + side] = first
        gram_ref[at + side : at + half, at : at + side] = cross
        gram_ref[at : at + side, at + side : at + half] = cross.T
        gram_ref[at + side : at + half, at + side : at + half] = second
    off = jnp.concatenate([pieces_ref[d, own:] for d in range(2 * sensor)], axis=0)
    for part in range(2):
        block = off[part * half : (part + 1) * half]
        gram_ref[:half, half + part * side : half + (part + 1) * side] = block
        gram_ref[half + part * side : half + (part + 1) * side, :half] = block.T


def finish_kernel(
    own, count, day_ref, pieces_ref, start_ref, *refs
):
    series, (day_basis_ref, core_ref) = refs[: count + 1], refs[count + 1 : count + 3]
    gram_ref, low_ref, own_ref, other_ref, done = refs[count + 3 :]
    copies = [pltpu.make_async_copy(series[0], own_ref, done.at[0])]
    at = 0
    for k, part in enumerate(series[1:]):
        here = part.shape[1]
        copies.append(
            pltpu.make_async_copy(part, other_ref.at[:, pl.ds(at, here), :], done.at[k + 1])
        )
        at += here
    for copy in copies:
        copy.start()
    join(pieces_ref.shape[0] // 2, own, pieces_ref, gram_ref)
    basis = lax.fori_loop(0, ITERS, lambda _, b: one_round(gram_ref, b), start_ref[...])
    finish(basis, day_basis_ref, low_ref)
    for copy in copies:
        copy.wait()
    components, days, _ = own_ref.shape
    rank = low_ref.shape[0]
    day = day_ref[0]
    own_basis, other_basis = (
        low_ref[:, pl.ds(pl.multiple_of(block * days, days), days)] for block in (day, 1 - day)
    )
    step = 128 // rank
    for c in range(0, components, step):
        values = []
        for k in range(c, c + step):
            both = jnp.dot(own_basis, own_ref[k], preferred_element_type=jnp.float32)
            both += jnp.dot(other_basis, other_ref[k], preferred_element_type=jnp.float32)
            values.append(both)
        turned = jnp.concatenate(values, axis=0).T
        core_ref[:, c * rank : (c + step) * rank] = turned.astype(jnp.bfloat16)


WHOLE = pl.BlockSpec(memory_space=pltpu.VMEM)
SCALAR = pl.BlockSpec(memory_space=pltpu.SMEM)
VMEM_LIMIT = 24 * 1024 * 1024


def basis_shapes(start):
    return (
        jax.ShapeDtypeStruct(start.shape, jnp.float32),
        jax.ShapeDtypeStruct(start.shape, jnp.bfloat16),
    )


def rounds(gram, start):
    return pl.pallas_call(
        rounds_kernel,
        out_shape=basis_shapes(start),
        in_specs=[WHOLE, WHOLE],
        out_specs=(WHOLE, WHOLE),
        name="rounds",
    )(gram, start)


def finish_pairs(day, pieces, own, start, series, parts):
    rank, days_all = start.shape
    components, days, sensors = series.shape
    anywhere = pl.BlockSpec(memory_space=pltpu.HBM)
    regrouped = pltpu.VMEM((components, days, sensors), jnp.bfloat16)
    return pl.pallas_call(
        functools.partial(finish_kernel, own, len(parts)),
        out_shape=(
            jax.ShapeDtypeStruct(start.shape, jnp.float32),
            jax.ShapeDtypeStruct((sensors, components * rank), jnp.bfloat16),
        ),
        in_specs=[SCALAR, WHOLE, WHOLE, anywhere, *(anywhere for _ in parts)],
        out_specs=(WHOLE, WHOLE),
        scratch_shapes=[
            pltpu.VMEM((days_all, days_all), jnp.float32),
            pltpu.VMEM(start.shape, jnp.bfloat16),
            regrouped,
            regrouped,
            pltpu.SemaphoreType.DMA((len(parts) + 1,)),
        ],
        compiler_params=pltpu.CompilerParams(vmem_limit_bytes=VMEM_LIMIT),
        name="finish",
    )(
        day,
        pieces,
        start,
        *(pltpu.with_memory_space_constraint(array, pltpu.HBM) for array in (series, *parts)),
    )


GROUP = 8


def components_first(traffic, components, put):
    width = GROUP * components
    sensors = traffic.shape[0]
    row = lax.broadcasted_iota(jnp.int32, (width, width), 0)
    lane = lax.broadcasted_iota(jnp.int32, (width, width), 1)
    order = (row % GROUP) * components + row // GROUP == lane
    order = jnp.where(order, 1.0, 0.0).astype(jnp.bfloat16)
    for pair in range(traffic.shape[1] // (2 * width)):
        parts = []
        for at in (2 * pair * width, (2 * pair + 1) * width):
            turned = lax.dot_general(
                order,
                traffic[:, at : at + width],
                (((1,), (1,)), ((), ())),
                preferred_element_type=jnp.float32,
            )
            parts.append(turned.reshape(components, GROUP, sensors))
        put(2 * GROUP * pair, jnp.concatenate(parts, axis=1).astype(jnp.bfloat16))


def paired_dot(left_ref, right_ref):
    components, _, sensors = left_ref.shape
    step = max(1, 256 // sensors)
    total = None
    for at in range(0, components, step):
        left, right = (
            jnp.concatenate([ref[c] for c in range(at, at + step)], axis=1)
            for ref in (left_ref, right_ref)
        )
        term = lax.dot_general(
            left, right, (((1,), (1,)), ((), ())), preferred_element_type=jnp.float32
        )
        total = term if total is None else total + term
    return total


def local_kernel(day_ref, traffic_ref, series_ref, packed_ref, all_ref):
    def put(day, values):
        all_ref[:, day : day + values.shape[1], :] = values

    components_first(traffic_ref, all_ref.shape[0], put)
    sensors = series_ref.shape[2]
    series_ref[...] = all_ref[:, :, pl.ds(pl.multiple_of(day_ref[0] * sensors, sensors), sensors)]
    gram = paired_dot(all_ref, all_ref)
    side = gram.shape[0] // 2
    packed_ref[:side] = gram[:side, :side]
    packed_ref[side : 2 * side] = gram[side:, :side]
    packed_ref[2 * side :] = gram[side:, side:]


def local(day, traffic, days, components):
    sensors = traffic.shape[0]
    side = days // 2
    return pl.pallas_call(
        local_kernel,
        out_shape=(
            jax.ShapeDtypeStruct((components, days, sensors // 2), jnp.bfloat16),
            jax.ShapeDtypeStruct((3 * side, side), jnp.float32),
        ),
        in_specs=[SCALAR, WHOLE],
        out_specs=(WHOLE, WHOLE),
        scratch_shapes=[pltpu.VMEM((components, days, sensors), jnp.bfloat16)],
        compiler_params=pltpu.CompilerParams(vmem_limit_bytes=VMEM_LIMIT),
        cost_estimate=pl.CostEstimate(
            flops=2 * traffic.size * (days + 256), bytes_accessed=4 * traffic.size, transcendentals=0
        ),
        name="local",
    )(day, traffic)


def arrived_kernel(first, day_ref, traffic_ref, series_ref, *refs):
    arrived_ref, gram_ref = refs[-2:]
    for before_ref in refs[:-2]:
        gram_ref[...] = before_ref[...]

    def put(day, values):
        arrived_ref[:, day : day + values.shape[1], :] = values

    components_first(traffic_ref, series_ref.shape[0], put)
    here, days, side = arrived_ref.shape[1], series_ref.shape[1], gram_ref.shape[1]

    @pl.when(day_ref[0] == 0)
    def _():
        gram = paired_dot(series_ref, arrived_ref)
        row, lane = first // side * days, first % side
        gram_ref[row : row + days, lane : lane + here] = gram

    @pl.when(day_ref[0] != 0)
    def _():
        gram = paired_dot(arrived_ref, series_ref)
        for part in range(days // side):
            row = part * days + first
            gram_ref[row : row + here, :] = gram[:, part * side : (part + 1) * side]


def arrived(day, traffic, series, gram, first):
    components, days, sensors = series.shape
    here = traffic.shape[1] // components
    side = days // 2
    before = () if gram is None else (gram,)
    return pl.pallas_call(
        functools.partial(arrived_kernel, first),
        out_shape=(
            jax.ShapeDtypeStruct((components, here, sensors), jnp.bfloat16),
            jax.ShapeDtypeStruct((2 * days, side), jnp.float32),
        ),
        in_specs=[SCALAR, WHOLE, WHOLE, *(WHOLE for _ in before)],
        out_specs=(WHOLE, WHOLE),
        compiler_params=pltpu.CompilerParams(vmem_limit_bytes=VMEM_LIMIT),
        cost_estimate=pl.CostEstimate(
            flops=2 * traffic.size * (days + 256), bytes_accessed=4 * traffic.size, transcendentals=0
        ),
        name="arrived",
    )(day, traffic, series, *before)


def scatter_sum(values, axes):
    devices = lax.axis_size(axes)
    pieces = values.reshape(devices, values.shape[0] // devices, values.shape[1])
    return jnp.sum(lax.all_to_all(pieces, axes, split_axis=0, concat_axis=0, tiled=True), axis=0)


def gather(piece, axes):
    copies = jnp.broadcast_to(piece, (lax.axis_size(axes), *piece.shape))
    return lax.all_to_all(copies, axes, split_axis=0, concat_axis=0, tiled=True)


def sum_over_devices(local, axes):
    flat = local.reshape(local.size // 128, 128)
    return gather(scatter_sum(flat, axes), axes).reshape(local.shape)


def shards(traffic, start_basis):
    regrouped = lax.all_to_all(traffic, "day", split_axis=0, concat_axis=1, tiled=True)
    sensors_here = regrouped.shape[0]
    days_all = start_basis.shape[0]
    components = regrouped.shape[1] // days_all
    series = regrouped.reshape(sensors_here, days_all, components)
    gram_local = lax.dot_general(
        series, series, (((0, 2), (0, 2)), ((), ())), preferred_element_type=jnp.float32
    )
    gram = sum_over_devices(gram_local, AXES)
    day_basis, basis_low = rounds(gram, start_basis.T)
    core = jnp.einsum("sdt,rd->str", series, basis_low, preferred_element_type=jnp.float32).astype(
        jnp.bfloat16
    )
    return (day_basis.T, core.reshape(sensors_here, components * basis_low.shape[0]))


CHUNKS = 4


def paired_shards(traffic, start_basis):
    days = start_basis.shape[0] // 2
    components = traffic.shape[1] // days
    sensors = traffic.shape[0] // 2
    day = lax.axis_index("day")
    index = day.astype(jnp.int32).reshape(1)
    wide = traffic.shape[1] // CHUNKS
    row = (1 - day) * sensors
    chunks = []
    for at in range(CHUNKS):
        wanted = lax.dynamic_slice(traffic, (row, at * wide), (sensors, wide))
        if at == 0:
            wanted, row = lax.optimization_barrier((wanted, row))
        chunks.append(lax.ppermute(wanted, "day", [(0, 1), (1, 0)]))
    series, packed = local(index, traffic, days, components)
    own = scatter_sum(packed, "sensor")
    parts, off = [], None
    for at, chunk in enumerate(chunks):
        part, off = arrived(index, chunk, series, off, at * days // CHUNKS)
        parts.append(part)
    pieces = gather(jnp.concatenate([own, scatter_sum(off, AXES)], axis=0), AXES)
    day_basis, core = finish_pairs(index, pieces, own.shape[0], start_basis.T, series, parts)
    return (day_basis.T, core)


def pairs(mesh):
    return mesh.shape["day"] == 2


def solution(mesh):
    placed = (P("sensor", "day"), P())
    return jax.shard_map(
        paired_shards if pairs(mesh) else shards,
        mesh=mesh,
        in_specs=placed,
        out_specs=(P(), P(AXES, None)),
        check_vma=False,
    )
```

```python
import functools

import jax
import jax.numpy as jnp
from jax import lax
from jax.experimental import pallas as pl
from jax.experimental.pallas import tpu as pltpu
from jax.sharding import PartitionSpec as P

ITERS = 3
AXES = ("sensor", "day")


def dot32(left, right, dims):
    return lax.dot_general(
        left,
        right,
        (dims, ((), ())),
        precision=lax.Precision.HIGHEST,
        preferred_element_type=jnp.float32,
    )


def inverse_factor(product, width=8):
    rank = product.shape[0]
    rows_at = lax.broadcasted_iota(jnp.int32, (rank, rank), 0)
    lanes_at = lax.broadcasted_iota(jnp.int32, (rank, rank), 1)
    unit = jnp.where(rows_at == lanes_at, 1.0, 0.0).astype(jnp.float32)
    both = jnp.concatenate([product, unit], axis=1)
    panels = [both[at : at + width] for at in range(0, rank, width)]
    row_of = lax.broadcasted_iota(jnp.int32, (width, 2 * rank), 0)

    def spread(values):
        return jnp.broadcast_to(values, (width, 2 * rank))

    done = []
    for here in range(rank // width):
        base = here * width
        below = range(here + 1, rank // width)
        rows = [spread(panels[here][w : w + 1]) for w in range(width)]
        pivots = {
            (v, w): spread(rows[v][:, base + w : base + w + 1])
            for v in range(width)
            for w in range(v, width)
        }
        columns = {
            (i, w): spread(panels[i][:, base + w : base + w + 1])
            for i in below
            for w in range(width)
        }
        for v in range(width):
            scale = lax.rsqrt(pivots[v, v])
            rows[v] = rows[v] * scale
            for w in range(v + 1, width):
                pivots[v, w] = pivots[v, w] * scale
            for i in below:
                columns[i, v] = columns[i, v] * scale
            for w in range(v + 1, width):
                for x in range(w, width):
                    pivots[w, x] = pivots[w, x] - pivots[v, w] * pivots[v, x]
                rows[w] = rows[w] - pivots[v, w] * rows[v]
                for i in below:
                    columns[i, w] = columns[i, w] - pivots[v, w] * columns[i, v]
            for i in below:
                panels[i] = panels[i] - columns[i, v] * rows[v]
        panel = rows[0]
        for w in range(1, width):
            panel = jnp.where(row_of == w, rows[w], panel)
        done.append(panel)
    return jnp.concatenate(done, axis=0)[:, rank:]


def one_round(gram_ref, basis):
    images = dot32(basis, gram_ref[...], ((1,), (0,)))
    product = dot32(images, images, ((1,), (1,)))
    return dot32(inverse_factor(product), images, ((1,), (0,)))


def finish(basis, day_basis_ref, low_ref):
    day_basis_ref[...] = basis * jnp.sqrt(jnp.float32(basis.shape[1]))
    low_ref[...] = basis.astype(jnp.bfloat16)


def rounds_kernel(gram_ref, start_ref, day_basis_ref, low_ref):
    basis = lax.fori_loop(0, ITERS, lambda _, b: one_round(gram_ref, b), start_ref[...])
    finish(basis, day_basis_ref, low_ref)


def join(sensor, own, pieces_ref, gram_ref):
    half = gram_ref.shape[0] // 2
    side = half // 2
    for day in range(2):
        packed = jnp.concatenate([pieces_ref[2 * s + day, :own] for s in range(sensor)], axis=0)
        first, cross, second = packed[:side], packed[side : 2 * side], packed[2 * side :]
        at = day * half
        gram_ref[at : at + side, at : at + side] = first
        gram_ref[at + side : at + half, at : at + side] = cross
        gram_ref[at : at + side, at + side : at + half] = cross.T
        gram_ref[at + side : at + half, at + side : at + half] = second
    off = jnp.concatenate([pieces_ref[d, own:] for d in range(2 * sensor)], axis=0)
    for part in range(2):
        block = off[part * half : (part + 1) * half]
        gram_ref[:half, half + part * side : half + (part + 1) * side] = block
        gram_ref[half + part * side : half + (part + 1) * side, :half] = block.T


def finish_kernel(
    own, count, day_ref, pieces_ref, start_ref, *refs
):
    series, (day_basis_ref, core_ref) = refs[: count + 1], refs[count + 1 : count + 3]
    gram_ref, low_ref, own_ref, other_ref, done = refs[count + 3 :]
    copies = [pltpu.make_async_copy(series[0], own_ref, done.at[0])]
    at = 0
    for k, part in enumerate(series[1:]):
        here = part.shape[1]
        copies.append(
            pltpu.make_async_copy(part, other_ref.at[:, pl.ds(at, here), :], done.at[k + 1])
        )
        at += here
    for copy in copies:
        copy.start()
    join(pieces_ref.shape[0] // 2, own, pieces_ref, gram_ref)
    basis = lax.fori_loop(0, ITERS, lambda _, b: one_round(gram_ref, b), start_ref[...])
    finish(basis, day_basis_ref, low_ref)
    for copy in copies:
        copy.wait()
    components, days, _ = own_ref.shape
    rank = low_ref.shape[0]
    day = day_ref[0]
    own_basis, other_basis = (
        low_ref[:, pl.ds(pl.multiple_of(block * days, days), days)] for block in (day, 1 - day)
    )
    step = 128 // rank
    for c in range(0, components, step):
        values = []
        for k in range(c, c + step):
            both = jnp.dot(own_basis, own_ref[k], preferred_element_type=jnp.float32)
            both += jnp.dot(other_basis, other_ref[k], preferred_element_type=jnp.float32)
            values.append(both)
        turned = jnp.concatenate(values, axis=0).T
        core_ref[:, c * rank : (c + step) * rank] = turned.astype(jnp.bfloat16)


WHOLE = pl.BlockSpec(memory_space=pltpu.VMEM)
SCALAR = pl.BlockSpec(memory_space=pltpu.SMEM)
OUTSIDE = pl.BlockSpec(memory_space=pltpu.HBM)
VMEM_LIMIT = 24 * 1024 * 1024


def basis_shapes(start):
    return (
        jax.ShapeDtypeStruct(start.shape, jnp.float32),
        jax.ShapeDtypeStruct(start.shape, jnp.bfloat16),
    )


def rounds(gram, start):
    return pl.pallas_call(
        rounds_kernel,
        out_shape=basis_shapes(start),
        in_specs=[WHOLE, WHOLE],
        out_specs=(WHOLE, WHOLE),
        name="rounds",
    )(gram, start)


def finish_pairs(day, pieces, own, start, series, parts):
    rank, days_all = start.shape
    components, days, sensors = series.shape
    regrouped = pltpu.VMEM((components, days, sensors), jnp.bfloat16)
    return pl.pallas_call(
        functools.partial(finish_kernel, own, len(parts)),
        out_shape=(
            jax.ShapeDtypeStruct(start.shape, jnp.float32),
            jax.ShapeDtypeStruct((sensors, components * rank), jnp.bfloat16),
        ),
        in_specs=[SCALAR, WHOLE, WHOLE, OUTSIDE, *(OUTSIDE for _ in parts)],
        out_specs=(WHOLE, WHOLE),
        scratch_shapes=[
            pltpu.VMEM((days_all, days_all), jnp.float32),
            pltpu.VMEM(start.shape, jnp.bfloat16),
            regrouped,
            regrouped,
            pltpu.SemaphoreType.DMA((len(parts) + 1,)),
        ],
        compiler_params=pltpu.CompilerParams(vmem_limit_bytes=VMEM_LIMIT),
        name="finish",
    )(
        day,
        pieces,
        start,
        *(pltpu.with_memory_space_constraint(array, pltpu.HBM) for array in (series, *parts)),
    )


GROUP = 8


def components_first(traffic, components, put):
    width = GROUP * components
    sensors = traffic.shape[0]
    row = lax.broadcasted_iota(jnp.int32, (width, width), 0)
    lane = lax.broadcasted_iota(jnp.int32, (width, width), 1)
    order = (row % GROUP) * components + row // GROUP == lane
    order = jnp.where(order, 1.0, 0.0).astype(jnp.bfloat16)
    for pair in range(traffic.shape[1] // (2 * width)):
        parts = []
        for at in (2 * pair * width, (2 * pair + 1) * width):
            turned = lax.dot_general(
                order,
                traffic[:, at : at + width],
                (((1,), (1,)), ((), ())),
                preferred_element_type=jnp.float32,
            )
            parts.append(turned.reshape(components, GROUP, sensors))
        put(2 * GROUP * pair, jnp.concatenate(parts, axis=1).astype(jnp.bfloat16))


def paired_dot(left_ref, right_ref):
    components, _, sensors = left_ref.shape
    step = max(1, 256 // sensors)
    total = None
    for at in range(0, components, step):
        left, right = (
            jnp.concatenate([ref[c] for c in range(at, at + step)], axis=1)
            for ref in (left_ref, right_ref)
        )
        term = lax.dot_general(
            left, right, (((1,), (1,)), ((), ())), preferred_element_type=jnp.float32
        )
        total = term if total is None else total + term
    return total


def local_kernel(day_ref, traffic_ref, series_ref, packed_ref, all_ref):
    def put(day, values):
        all_ref[:, day : day + values.shape[1], :] = values

    components_first(traffic_ref, all_ref.shape[0], put)
    sensors = series_ref.shape[2]
    series_ref[...] = all_ref[:, :, pl.ds(pl.multiple_of(day_ref[0] * sensors, sensors), sensors)]
    gram = paired_dot(all_ref, all_ref)
    side = gram.shape[0] // 2
    packed_ref[:side] = gram[:side, :side]
    packed_ref[side : 2 * side] = gram[side:, :side]
    packed_ref[2 * side :] = gram[side:, side:]


def local(day, traffic, days, components):
    sensors = traffic.shape[0]
    side = days // 2
    return pl.pallas_call(
        local_kernel,
        out_shape=(
            jax.ShapeDtypeStruct((components, days, sensors // 2), jnp.bfloat16),
            jax.ShapeDtypeStruct((3 * side, side), jnp.float32),
        ),
        in_specs=[SCALAR, WHOLE],
        out_specs=(WHOLE, WHOLE),
        scratch_shapes=[pltpu.VMEM((components, days, sensors), jnp.bfloat16)],
        compiler_params=pltpu.CompilerParams(vmem_limit_bytes=VMEM_LIMIT),
        cost_estimate=pl.CostEstimate(
            flops=2 * traffic.size * (days + 256), bytes_accessed=4 * traffic.size, transcendentals=0
        ),
        name="local",
    )(day, traffic)


def arrived_kernel(first, day_ref, traffic_ref, series_ref, *refs):
    out_ref, gram_ref, arrived_ref, done = refs[-4:]
    for before_ref in refs[:-4]:
        gram_ref[...] = before_ref[...]

    def put(day, values):
        arrived_ref[:, day : day + values.shape[1], :] = values

    components_first(traffic_ref, series_ref.shape[0], put)
    out = pltpu.make_async_copy(arrived_ref, out_ref, done)
    out.start()
    here, days, side = arrived_ref.shape[1], series_ref.shape[1], gram_ref.shape[1]

    @pl.when(day_ref[0] == 0)
    def _():
        gram = paired_dot(series_ref, arrived_ref)
        row, lane = first // side * days, first % side
        gram_ref[row : row + days, lane : lane + here] = gram

    @pl.when(day_ref[0] != 0)
    def _():
        gram = paired_dot(arrived_ref, series_ref)
        for part in range(days // side):
            row = part * days + first
            gram_ref[row : row + here, :] = gram[:, part * side : (part + 1) * side]

    out.wait()


def arrived(day, traffic, series, gram, first):
    components, days, sensors = series.shape
    here = traffic.shape[1] // components
    side = days // 2
    before = () if gram is None else (gram,)
    return pl.pallas_call(
        functools.partial(arrived_kernel, first),
        out_shape=(
            pltpu.HBM((components, here, sensors), jnp.bfloat16),
            jax.ShapeDtypeStruct((2 * days, side), jnp.float32),
        ),
        in_specs=[SCALAR, WHOLE, WHOLE, *(WHOLE for _ in before)],
        out_specs=(OUTSIDE, WHOLE),
        scratch_shapes=[
            pltpu.VMEM((components, here, sensors), jnp.bfloat16),
            pltpu.SemaphoreType.DMA,
        ],
        compiler_params=pltpu.CompilerParams(vmem_limit_bytes=VMEM_LIMIT),
        cost_estimate=pl.CostEstimate(
            flops=2 * traffic.size * (days + 256), bytes_accessed=4 * traffic.size, transcendentals=0
        ),
        name="arrived",
    )(day, traffic, series, *before)


def scatter_sum(values, axes):
    devices = lax.axis_size(axes)
    pieces = values.reshape(devices, values.shape[0] // devices, values.shape[1])
    return jnp.sum(lax.all_to_all(pieces, axes, split_axis=0, concat_axis=0, tiled=True), axis=0)


def gather(piece, axes):
    copies = jnp.broadcast_to(piece, (lax.axis_size(axes), *piece.shape))
    return lax.all_to_all(copies, axes, split_axis=0, concat_axis=0, tiled=True)


def sum_over_devices(local, axes):
    flat = local.reshape(local.size // 128, 128)
    return gather(scatter_sum(flat, axes), axes).reshape(local.shape)


def shards(traffic, start_basis):
    regrouped = lax.all_to_all(traffic, "day", split_axis=0, concat_axis=1, tiled=True)
    sensors_here = regrouped.shape[0]
    days_all = start_basis.shape[0]
    components = regrouped.shape[1] // days_all
    series = regrouped.reshape(sensors_here, days_all, components)
    gram_local = lax.dot_general(
        series, series, (((0, 2), (0, 2)), ((), ())), preferred_element_type=jnp.float32
    )
    gram = sum_over_devices(gram_local, AXES)
    day_basis, basis_low = rounds(gram, start_basis.T)
    core = jnp.einsum("sdt,rd->str", series, basis_low, preferred_element_type=jnp.float32).astype(
        jnp.bfloat16
    )
    return (day_basis.T, core.reshape(sensors_here, components * basis_low.shape[0]))


def cut_kernel(first, row_ref, traffic_ref, *refs):
    outs, done = refs[:-1], refs[-1]
    copies = []
    at = first
    for k, out in enumerate(outs):
        sensors, wide = out.shape
        rows = pl.ds(pl.multiple_of(row_ref[0] * sensors, sensors), sensors)
        copies.append(
            pltpu.make_async_copy(traffic_ref.at[rows, pl.ds(at, wide)], out, done.at[k])
        )
        at += wide
    for copy in copies:
        copy.start()
    for copy in copies:
        copy.wait()


def cut(block, traffic, sensors, first, widths):
    return pl.pallas_call(
        functools.partial(cut_kernel, first),
        out_shape=tuple(jax.ShapeDtypeStruct((sensors, wide), traffic.dtype) for wide in widths),
        in_specs=[SCALAR, OUTSIDE],
        out_specs=tuple(WHOLE for _ in widths),
        scratch_shapes=[pltpu.SemaphoreType.DMA((len(widths),))],
        compiler_params=pltpu.CompilerParams(vmem_limit_bytes=VMEM_LIMIT),
        cost_estimate=pl.CostEstimate(
            flops=0, bytes_accessed=4 * sensors * sum(widths), transcendentals=0
        ),
        name="cut",
    )(block, pltpu.with_memory_space_constraint(traffic, pltpu.HBM))


CHUNKS = 4


def paired_shards(traffic, start_basis):
    days = start_basis.shape[0] // 2
    components = traffic.shape[1] // days
    sensors = traffic.shape[0] // 2
    day = lax.axis_index("day")
    index = day.astype(jnp.int32).reshape(1)
    wide = traffic.shape[1] // CHUNKS
    chunks = []
    for first, count in ((0, 1), (1, CHUNKS - 1)):
        for wanted in cut(1 - index, traffic, sensors, first * wide, [wide] * count):
            chunks.append(lax.ppermute(wanted, "day", [(0, 1), (1, 0)]))
    series, packed = local(index, traffic, days, components)
    own = scatter_sum(packed, "sensor")
    parts, off = [], None
    for at, chunk in enumerate(chunks):
        part, off = arrived(index, chunk, series, off, at * days // CHUNKS)
        parts.append(part)
    pieces = gather(jnp.concatenate([own, scatter_sum(off, AXES)], axis=0), AXES)
    day_basis, core = finish_pairs(index, pieces, own.shape[0], start_basis.T, series, parts)
    return (day_basis.T, core)


def pairs(mesh):
    return mesh.shape["day"] == 2


def solution(mesh):
    placed = (P("sensor", "day"), P())
    return jax.shard_map(
        paired_shards if pairs(mesh) else shards,
        mesh=mesh,
        in_specs=placed,
        out_specs=(P(), P(AXES, None)),
        check_vma=False,
    )
```
